256 devices in a mesh: op: 8 (over z_lo, core), sec: 32 (over y, x, z_hi).
Axes of the slice: x: 4, y: 4, z: 8 (z_hi: 2, z_lo: 4; z = z_hi * 4 + z_lo), core: 2. Of those that a mesh axis runs over, the one named last changes fastest.
Arguments:
- psi: bfloat16 [3, 256, 256, 256], P(None, 'sec'), may hold values from -6 to 6
- left_ops: bfloat16 [32, 256, 256, 256], P('op', 'sec'), may hold values from -0.0625 to 0.0625
- right_ops: bfloat16 [32, 256, 256, 256], P('op', 'sec'), may hold values from -0.375 to 0.375
- shifts: int32 [32], P('op'), may hold values from -1 to 1
- active: int32 [32, 256], P('op', 'sec'), may hold values 0 or 1
Outputs:
- right_view: bfloat16 [3, 256, 256, 256], P(None, 'sec', None, 'op')
The draws below stay inside these ranges and needn't reach their ends.
All inputs are finite; a program needn't handle non-finite values. No bound on the sum of `active` on one device may be relied on, other than what follows from the above.
Results may differ from the reference program's by a relative error of at most 0.0049.
Values may be sent and summed in bfloat16 or wider, within the bound.
A program may use at most 64 MiB of HBM per device.

```python
import jax
import jax.numpy as jnp
from jax import lax

BLK = 256
NVEC = 3
QMAX = 1
TERMS = 32
NSEC = 256


def with_ends(array, rng, least, high):
    dims = array.shape
    index_at = [jax.random.randint(jax.random.fold_in(rng, axis), (), 0, dims[axis]) for axis in range(len(dims))]
    array = array.at[tuple(index_at)].set(least)
    longest = dims.index(max(dims))
    index_at[longest] = (index_at[longest] + 1) % dims[longest]
    return array.at[tuple(index_at)].set(high)


def block_levels(rng, shape, pieces, low, high):
    factor_of = 1.0
    for axis_at, blocks in pieces:
        heights = jax.random.uniform(jax.random.fold_in(jax.random.fold_in(rng, 6), axis_at), (blocks,), jnp.float32, low / len(pieces), high / len(pieces))
        factor_of = factor_of * jnp.repeat(jnp.exp(heights), shape[axis_at] // blocks).reshape((-1,) + (1,) * (len(shape) - 1 - axis_at))
    return factor_of


def centred(stream_key, dims, deviation, limit, split=(), held_as=jnp.bfloat16):
    level = block_levels(stream_key, dims, split, -0.22, 0.18) if split else 1.0
    values = jax.random.normal(stream_key, dims, jnp.float32) * deviation * level
    return jnp.minimum(jnp.maximum(values, -limit), limit).astype(held_as)


def setup_inputs(seed: int = 0) -> dict:
    splits = jax.random.split(jax.random.key(seed), 6)
    return {
        "psi": centred(splits[0], (NVEC, NSEC, BLK, BLK), 1.0, 6.0, ((1, 32),)),
        "left_ops": centred(splits[1], (TERMS, NSEC, BLK, BLK), (BLK * TERMS) ** -0.5, 0.0625, ((0, 8), (1, 32))),
        "right_ops": centred(splits[2], (TERMS, NSEC, BLK, BLK), BLK ** -0.5, 0.375, ((0, 8), (1, 32))),
        "shifts": with_ends(jax.random.randint(splits[3], (TERMS,), 0 - QMAX, QMAX + 1), jax.random.fold_in(splits[3], 1), 0 - QMAX, QMAX).astype(jnp.int32),
        "active": with_ends((jax.random.randint(splits[4], (TERMS, NSEC), 0, 4) < 3).astype(jnp.int32), jax.random.fold_in(splits[4], 1), 0, 1),
    }


def reference(psi, left_ops, right_ops, shifts, active):
    sectors = jnp.arange(NSEC, dtype=jnp.int32)

    def step(total, items):
        left, right, shift, mask = items
        anchor = (sectors - shift).astype(jnp.int32)
        valid = (anchor >= 0) & (anchor < NSEC)
        picked = jnp.take(psi, jnp.clip(anchor, 0, NSEC - 1).astype(jnp.int32), axis=1).astype(jnp.float32)
        source = jnp.where(valid[None, :, None, None], picked, jnp.float32(0.0))
        middle = jnp.einsum("tij,vtjk->vtik", left.astype(jnp.float32), source).astype(jnp.bfloat16)
        middle = lax.optimization_barrier(middle).astype(jnp.float32)
        term = jnp.einsum("vtik,tlk->vlti", middle, right.astype(jnp.float32))
        weight = mask.astype(jnp.float32)
        return total + term * weight[None, None, :, None], None

    start = jnp.zeros((NVEC, BLK, NSEC, BLK), jnp.float32)
    total, _ = lax.scan(step, start, (left_ops, right_ops, shifts, active))
    return total.astype(jnp.bfloat16)
```

```python
import functools

import jax
import jax.numpy as jnp
from jax import lax
from jax.experimental import pallas as pl
from jax.experimental.pallas import tpu as pltpu
from jax.sharding import PartitionSpec as P

MESH = pl.DeviceIdType.MESH
F32 = jnp.float32
BF16 = jnp.bfloat16
LAG = 2


def kernel(
    nsec_total, sizes, shifts, active, psi_hbm, left_hbm, right_hbm, out_ref,
    psi, edge, left, right, perm, mid, rcat, acc,
    s0, r0, s1, keep, r1, s2, own, r2, turn, wide, wsend, wrecv,
    load_sem, op_sem, edge_sem, halo_send, halo_recv, sib_send, sib_recv,
    send0, recv0, send1, recv1, send2, recv2, send3, recv3, self_sem,
):
    nyx, count, nvec, sectors, blk = sizes
    op, sec = lax.axis_index("op"), lax.axis_index("sec")
    zl, core = lax.div(op, 2), lax.rem(op, 2)
    yx, zh = lax.div(sec, 2), lax.rem(sec, 2)
    z = zh * 4 + zl
    e = lax.rem(zl, 2)
    other = 1 - core
    nsec = 2 * nyx
    half = blk // 2

    def at(zz, yxx):
        zz = lax.rem(zz + 16, 8)
        return {"op": lax.rem(zz, 4) * 2 + core, "sec": yxx * 2 + lax.div(zz, 4)}

    sibling = {"op": zl * 2 + other, "sec": sec}
    partner = at(z + 1 - 2 * e, yx)
    sec_up, sec_down = lax.rem(sec + 1, nsec), lax.rem(sec + nsec - 1, nsec)
    ahead = {
        "op": jnp.where(zl == 3, core, op + 2),
        "sec": jnp.where(zl == 3, sec_up, sec),
    }
    behind = {
        "op": jnp.where(zl == 0, 6 + core, op - 2),
        "sec": jnp.where(zl == 0, sec_down, sec),
    }

    barrier = pltpu.get_barrier_semaphore()
    pl.semaphore_signal(barrier, inc=1, device_id=sibling, device_id_type=MESH)
    pl.semaphore_signal(barrier, inc=1, device_id=ahead, device_id_type=MESH)
    pl.semaphore_signal(barrier, inc=1, device_id=behind, device_id_type=MESH)

    @pl.loop(1, 8)
    def _(d):
        pl.semaphore_signal(barrier, inc=1, device_id=at(z + d, yx), device_id_type=MESH)

    @pl.loop(1, nyx)
    def _(d):
        pl.semaphore_signal(
            barrier, inc=1, device_id=at(z, lax.rem(yx + d, nyx)), device_id_type=MESH
        )

    load_psi = pltpu.make_async_copy(psi_hbm, psi, load_sem)
    load_psi.start()

    def sector_of(n):
        return jnp.where(n < sectors - 2, n + 1, jnp.where(n == sectors - 2, 0, sectors - 1))

    def load_ops(t):
        return (
            pltpu.make_async_copy(left_hbm.at[:, t], left.at[t], op_sem.at[0, t]),
            pltpu.make_async_copy(right_hbm.at[:, t], right.at[t], op_sem.at[1, t]),
        )

    @pl.loop(0, sectors)
    def _(n):
        for copy in load_ops(sector_of(n)):
            copy.start()

    edge_loads = (
        pltpu.make_async_copy(psi_hbm.at[:, 0:2], edge.at[0, :, 1:3], edge_sem.at[0]),
        pltpu.make_async_copy(
            psi_hbm.at[:, sectors - 2 : sectors], edge.at[1, :, 0:2], edge_sem.at[1]
        ),
    )
    for copy in edge_loads:
        copy.start()

    rows_each = blk // nsec
    row = lax.broadcasted_iota(jnp.int32, (blk, blk), 0)
    col = lax.broadcasted_iota(jnp.int32, (blk, blk), 1)
    inner = lax.rem(row, half)
    want = (
        lax.div(inner, rows_each) * (2 * rows_each)
        + lax.div(row, half) * rows_each
        + lax.rem(inner, rows_each)
    )
    perm[...] = jnp.where(col == want, 1.0, 0.0).astype(BF16)

    load_psi.wait()
    pl.semaphore_wait(barrier, 3 + 7 + nyx - 1)

    mine = pl.ds(core * half, half)

    def halo(side, v, source):
        return pltpu.make_async_remote_copy(
            src_ref=source,
            dst_ref=edge.at[side, v, 2 * side, mine],
            send_sem=halo_send.at[side, v],
            recv_sem=halo_recv.at[side, v],
            device_id=behind if side else ahead,
            device_id_type=MESH,
        )

    def share(side, v):
        return pltpu.make_async_remote_copy(
            src_ref=edge.at[side, v, 2 * side, mine],
            dst_ref=edge.at[side, v, 2 * side, mine],
            send_sem=sib_send.at[side, v],
            recv_sem=sib_recv.at[side, v],
            device_id=sibling,
            device_id_type=MESH,
        )

    @pl.when(zl == 3)
    def _():
        for v in range(nvec):
            halo(0, v, psi.at[v, sectors - 1, mine]).start()

    @pl.when(zl == 0)
    def _():
        for v in range(nvec):
            halo(1, v, psi.at[v, 0, mine]).start()

    def relay(side, n):
        place = (3 - zl) if side else zl
        v = n - place

        @pl.when((v >= 0) & (v < nvec))
        def _():
            here = edge.at[side, v, 2 * side, mine]
            halo(side, v, here).wait_recv()

            @pl.when(place < 3)
            def _():
                halo(side, v, here).start()

            share(side, v).start()

    def compute(t, slot, source):
        for k in range(count):
            shift = shifts[k]
            anchor = sec * sectors + t - shift
            good = (anchor >= 0) & (anchor < nsec_total)
            weight = jnp.where(good, active[k, t], 0).astype(F32)
            moved = jnp.dot(perm[...], right[t, k], preferred_element_type=F32)
            rcat[:, k * blk : (k + 1) * blk] = (moved * weight).astype(BF16)
            for v in range(nvec):
                mid[v, :, k * blk : (k + 1) * blk] = jnp.dot(
                    left[t, k], source(v, shift), preferred_element_type=F32
                ).astype(BF16)
        for v in range(nvec):
            acc[slot, v] = lax.dot_general(
                mid[v], rcat[...], (((1,), (1,)), ((), ())), preferred_element_type=F32
            ).reshape(4, 2, blk // 8, blk)

    def level0(t):
        return pltpu.make_async_remote_copy(
            src_ref=s0.at[t], dst_ref=r0.at[t], send_sem=send0.at[t], recv_sem=recv0.at[t],
            device_id=sibling, device_id_type=MESH,
        )

    def level1(t):
        return pltpu.make_async_remote_copy(
            src_ref=s1.at[t, e], dst_ref=r1.at[t], send_sem=send1.at[t], recv_sem=recv1.at[t],
            device_id=partner, device_id_type=MESH,
        )

    def level2(t, p):
        return pltpu.make_async_remote_copy(
            src_ref=s2.at[t, p - 1], dst_ref=r2.at[p - 1, t],
            send_sem=send2.at[t, p - 1], recv_sem=recv2.at[t, p - 1],
            device_id=at(z + jnp.where(e == 1, p, -p), yx), device_id_type=MESH,
        )

    def stage0(t, slot):
        s0[t] = acc[slot, :, :, other].astype(BF16)
        level0(t).start()

    def stage1(t, slot):
        level0(t).wait_recv()
        for zl2 in range(4):
            for zh2 in range(2):
                lanes = slice(zh2 * half, (zh2 + 1) * half)
                value = acc[slot, :, zl2, core, :, lanes] + r0[t, :, zl2, :, lanes].astype(F32)
                delta = lax.rem(zh2 * 4 + zl2 - (z - e) + 16, 8)
                low = (delta >= 1) & (delta <= 4)
                side = jnp.where(low, 0, 1)
                place = jnp.where(low, delta - 1, lax.rem(8 - delta, 8))
                s1[t, side, place] = value.astype(BF16)
                keep[t, side, place] = value
        level1(t).start()

    def stage2(t):
        level1(t).wait_recv()
        for p in range(4):
            value = keep[t, 1 - e, p] + r1[t, p].astype(F32)
            if p == 0:
                own[t] = value
            else:
                s2[t, p - 1] = value.astype(BF16)
                level2(t, p).start()

    @pl.loop(0, sectors + LAG)
    def _(n):
        slot = lax.rem(n, 2)

        @pl.when(n < sectors)
        def _():
            t = sector_of(n)
            for copy in load_ops(t):
                copy.wait()

            @pl.when(n < sectors - 2)
            def _():
                compute(t, slot, lambda v, shift: psi[v, t - shift])

            @pl.when(n == sectors - 2)
            def _():
                for copy in edge_loads:
                    copy.wait()
                for side in range(2):
                    for v in range(nvec):
                        share(side, v).wait_recv()

            @pl.when(n >= sectors - 2)
            def _():
                which = n - (sectors - 2)
                compute(t, slot, lambda v, shift: edge[which, v, 1 - shift])

            stage0(t, slot)

        @pl.when(n < sectors - 2)
        def _():
            relay(0, n)
            relay(1, n)

        @pl.when((n >= 1) & (n <= sectors))
        def _():
            stage1(sector_of(n - 1), 1 - slot)

        @pl.when(n >= LAG)
        def _():
            stage2(sector_of(n - LAG))

    near = jnp.where(lax.rem(e + lax.div(zl, 2), 2) == 1, 0, 1)
    for p in range(1, 4):
        @pl.loop(0, sectors)
        def _(t):
            level2(t, p).wait_recv()

    part = blk // 8
    for mine_group in (True, False):
        group = zh if mine_group else 1 - zh

        @pl.loop(0, nvec)
        def _(v):
            for quad in range(2):
                ts = slice(quad * 4, quad * 4 + 4)
                if mine_group:
                    value = own[ts, v] + r2[near, ts, v].astype(F32)
                else:
                    value = r2[1 - near, ts, v].astype(F32) + r2[2, ts, v].astype(F32)
                turn[quad] = value.reshape(4 * part, half).T
                for lq in range(2):
                    pieces = [turn[quad, pl.ds(lq * 4 + r, nyx, stride=8), :] for r in range(4)]
                    for t4 in range(4):
                        lanes = slice(t4 * part, (t4 + 1) * part)
                        joined = jnp.concatenate([piece[:, lanes] for piece in pieces], axis=1)
                        wide[group, v * 2 + lq, pl.ds(quad * 4 + t4, nyx, stride=8), :] = joined

    @pl.loop(0, nyx)
    def _(d):
        rows = pl.ds(pl.multiple_of(d * 8, 8), 8)
        for tile in range(6):
            both = [wide[group, tile, rows, :] for group in range(2)]
            lanes = slice(tile * 128, (tile + 1) * 128)
            wsend[d, :, lanes] = jnp.concatenate(both, axis=0).astype(BF16)

    def spread(d):
        far = lax.rem(yx + d, nyx)
        return pltpu.make_async_remote_copy(
            src_ref=wsend.at[far], dst_ref=wrecv.at[yx],
            send_sem=send3.at[d], recv_sem=recv3.at[d],
            device_id=at(z, far), device_id_type=MESH,
        )

    @pl.loop(1, nyx)
    def _(d):
        spread(d).start()

    keep_own = pltpu.make_async_copy(wsend.at[yx], wrecv.at[yx], self_sem)
    keep_own.start()
    keep_own.wait()

    @pl.loop(1, nyx)
    def _(d):
        spread(d).wait_recv()

    for h in range(2):
        for tile in range(6):
            lanes = slice(tile * 128, (tile + 1) * 128)
            value = wrecv[h * 8 : (h + 1) * 8, :, lanes].astype(F32).reshape(128, 128)
            out_ref[lanes, h * 128 : (h + 1) * 128] = value.T.astype(BF16)

    for side in range(2):
        for v in range(nvec):
            halo(side, v, psi.at[v, 0, mine]).wait_send()
            share(side, v).wait_send()

    @pl.loop(0, sectors)
    def _(t):
        level0(t).wait_send()
        level1(t).wait_send()
        for p in range(1, 4):
            level2(t, p).wait_send()

    @pl.loop(1, nyx)
    def _(d):
        spread(d).wait_send()


def solution(mesh):
    nsec = mesh.shape["sec"]
    nyx = nsec // 2

    def per_device(psi, left_ops, right_ops, shifts, active):
        nvec, sectors, blk = psi.shape[:3]
        count = left_ops.shape[0]
        part, half = blk // 8, blk // 2
        sizes = (nyx, count, nvec, sectors, blk)
        smem = pl.BlockSpec(memory_space=pltpu.SMEM)
        hbm = pl.BlockSpec(memory_space=pl.ANY)
        dma = pltpu.SemaphoreType.DMA
        result = pl.pallas_call(
            functools.partial(kernel, nsec * sectors, sizes),
            out_shape=jax.ShapeDtypeStruct((nvec * blk, blk), BF16),
            in_specs=[smem, smem, hbm, hbm, hbm],
            out_specs=pl.BlockSpec(memory_space=pltpu.VMEM),
            scratch_shapes=[
                pltpu.VMEM((nvec, sectors, blk, blk), BF16),
                pltpu.VMEM((2, nvec, 3, blk, blk), BF16),
                pltpu.VMEM((sectors, count, blk, blk), BF16),
                pltpu.VMEM((sectors, count, blk, blk), BF16),
                pltpu.VMEM((blk, blk), BF16),
                pltpu.VMEM((nvec, blk, count * blk), BF16),
                pltpu.VMEM((blk, count * blk), BF16),
                pltpu.VMEM((2, nvec, 4, 2, part, blk), F32),
                pltpu.VMEM((sectors, nvec, 4, part, blk), BF16),
                pltpu.VMEM((sectors, nvec, 4, part, blk), BF16),
                pltpu.VMEM((sectors, 2, 4, nvec, part, half), BF16),
                pltpu.VMEM((sectors, 2, 4, nvec, part, half), F32),
                pltpu.VMEM((sectors, 4, nvec, part, half), BF16),
                pltpu.VMEM((sectors, 3, nvec, part, half), BF16),
                pltpu.VMEM((sectors, nvec, part, half), F32),
                pltpu.VMEM((3, sectors, nvec, part, half), BF16),
                pltpu.VMEM((2, 128, 128), F32),
                pltpu.VMEM((2, nvec * 2, nyx * 8, 128), F32),
                pltpu.VMEM((nyx, 16, nvec * blk), BF16),
                pltpu.VMEM((nyx, 16, nvec * blk), BF16),
                dma,
                dma((2, sectors)),
                dma((2,)),
                dma((2, nvec)), dma((2, nvec)), dma((2, nvec)), dma((2, nvec)),
                dma((sectors,)), dma((sectors,)), dma((sectors,)), dma((sectors,)),
                dma((sectors, 3)), dma((sectors, 3)),
                dma((nyx,)), dma((nyx,)),
                dma,
            ],
            compiler_params=pltpu.CompilerParams(
                collective_id=0, has_side_effects=True, vmem_limit_bytes=56 * 1024 * 1024
            ),
        )(shifts, active, psi, left_ops, right_ops)
        return result.reshape(nvec, blk // nsec, blk // 8, blk).transpose(0, 1, 3, 2)

    return jax.shard_map(
        per_device,
        mesh=mesh,
        in_specs=(
            P(None, "sec", None, None),
            P("op", "sec", None, None),
            P("op", "sec", None, None),
            P("op"),
            P("op", "sec"),
        ),
        out_specs=P(None, "sec", None, "op"),
        check_vma=False,
    )
```

```python
import functools

import jax
import jax.numpy as jnp
from jax import lax
from jax.experimental import pallas as pl
from jax.experimental.pallas import tpu as pltpu
from jax.sharding import PartitionSpec as P

MESH = pl.DeviceIdType.MESH
F32 = jnp.float32
BF16 = jnp.bfloat16
LAG = 4
RELAY = 2
EARLY = False


def kernel(
    nsec_total, sizes, shifts, active, psi_hbm, left_hbm, right_hbm, out_ref,
    psi, edge, left, right, perm, mid, rcat, acc,
    s0, r0, s1, keep, r1, s2, own, r2, turn, wide, wsend, wrecv, order, flat,
    load_sem, op_sem, edge_sem, halo_send, halo_recv, sib_send, sib_recv,
    send0, recv0, send1, recv1, send2, recv2, send3, recv3, self_sem,
):
    nyx, count, nvec, sectors, blk = sizes
    assert (nyx, sectors, blk) == (16, 8, 256)
    op, sec = lax.axis_index("op"), lax.axis_index("sec")
    zl, core = lax.div(op, 2), lax.rem(op, 2)
    yx, zh = lax.div(sec, 2), lax.rem(sec, 2)
    z = zh * 4 + zl
    e = lax.rem(zl, 2)
    other = 1 - core
    nsec = 2 * nyx
    half = blk // 2

    def at(zz, yxx):
        zz = lax.rem(zz + 16, 8)
        return {"op": lax.rem(zz, 4) * 2 + core, "sec": yxx * 2 + lax.div(zz, 4)}

    sibling = {"op": zl * 2 + other, "sec": sec}
    partner = at(z + 1 - 2 * e, yx)
    sec_up, sec_down = lax.rem(sec + 1, nsec), lax.rem(sec + nsec - 1, nsec)

    def chain(zls, secs):
        pick = lambda w: jnp.where(zl == 0, w[0], jnp.where(zl == 1, w[1], jnp.where(zl == 2, w[2], w[3])))
        return {"op": pick(zls) * 2 + core, "sec": pick(secs)}

    halo_to = (
        chain((2, 2, 1, 1), (sec_down, sec, sec, sec_up)),
        chain((3, 3, 0, 0), (sec_down, sec, sec, sec_up)),
        chain((3, 3, 0, 0), (sec_up, sec, sec, sec_down)),
    )
    greets = (
        chain((2, 3, 0, 1), (sec_down, sec_down, sec_up, sec_up)),
        chain((3, 2, 1, 0), (sec_down, sec, sec, sec_up)),
        chain((3, 2, 1, 0), (sec_up, sec, sec, sec_down)),
    )

    barrier = pltpu.get_barrier_semaphore()
    pl.semaphore_signal(barrier, inc=1, device_id=sibling, device_id_type=MESH)
    for peer in greets:
        pl.semaphore_signal(barrier, inc=1, device_id=peer, device_id_type=MESH)

    @pl.loop(1, 8)
    def _(d):
        pl.semaphore_signal(barrier, inc=1, device_id=at(z + d, yx), device_id_type=MESH)

    @pl.loop(1, nyx)
    def _(d):
        pl.semaphore_signal(
            barrier, inc=1, device_id=at(z, lax.rem(yx + d, nyx)), device_id_type=MESH
        )

    load_psi = pltpu.make_async_copy(psi_hbm, psi, load_sem)
    load_psi.start()

    def sector_of(n):
        return jnp.where(n < sectors - 2, n + 1, jnp.where(n == sectors - 2, 0, sectors - 1))

    def load_ops(t):
        return (
            pltpu.make_async_copy(left_hbm.at[:, t], left.at[t], op_sem.at[0, t]),
            pltpu.make_async_copy(right_hbm.at[:, t], right.at[t], op_sem.at[1, t]),
        )

    @pl.loop(0, sectors)
    def _(n):
        for copy in load_ops(sector_of(n)):
            copy.start()

    edge_loads = (
        pltpu.make_async_copy(psi_hbm.at[:, 0:2], edge.at[0, :, 1:3], edge_sem.at[0]),
        pltpu.make_async_copy(
            psi_hbm.at[:, sectors - 2 : sectors], edge.at[1, :, 0:2], edge_sem.at[1]
        ),
    )
    for copy in edge_loads:
        copy.start()

    row = lax.broadcasted_iota(jnp.int32, (blk, blk), 0)
    col = lax.broadcasted_iota(jnp.int32, (blk, blk), 1)
    want = ((row & 120) << 1) | ((row & 128) >> 4) | (row & 7)
    perm[...] = jnp.where(col == want, 1.0, 0.0).astype(BF16)

    turn_n = ((row & 128) >> 5) | (row & 3)
    sector = jnp.where(turn_n < 6, turn_n + 1, jnp.where(turn_n == 6, 0, 7))
    group = jnp.where(zh == 1, 1 - ((row & 4) >> 2), (row & 4) >> 2)
    order[...] = jnp.where(
        col == ((row & 120) << 1) + group * 8 + sector, 1.0, 0.0
    ).astype(BF16)


    mine = pl.ds(core * half, half)
    role = 1 - e

    def halo(side, v, hop, source):
        return pltpu.make_async_remote_copy(
            src_ref=source,
            dst_ref=edge.at[side, v, 2 * side, mine],
            send_sem=halo_send.at[hop, v],
            recv_sem=halo_recv.at[side, v],
            device_id=halo_to[hop],
            device_id_type=MESH,
        )

    def halo_in(side, v):
        return pltpu.make_async_remote_copy(
            src_ref=edge.at[side, v, 2 * side, mine],
            dst_ref=edge.at[side, v, 2 * side, mine],
            send_sem=halo_send.at[0, v],
            recv_sem=halo_recv.at[side, v],
            device_id=sibling,
            device_id_type=MESH,
        )

    def share(side):
        return pltpu.make_async_remote_copy(
            src_ref=edge.at[side, :, 2 * side, mine],
            dst_ref=edge.at[side, :, 2 * side, mine],
            send_sem=sib_send.at[side],
            recv_sem=sib_recv.at[side],
            device_id=sibling,
            device_id_type=MESH,
        )

    def compute(t, slot, source):
        for k in range(count):
            shift = shifts[k]
            anchor = sec * sectors + t - shift
            good = (anchor >= 0) & (anchor < nsec_total)
            weight = jnp.where(good, active[k, t], 0).astype(F32)
            moved = jnp.dot(perm[...], right[t, k], preferred_element_type=F32)
            rcat[:, k * blk : (k + 1) * blk] = (moved * weight).astype(BF16)
            for v in range(nvec):
                mid[v, :, k * blk : (k + 1) * blk] = jnp.dot(
                    left[t, k], source(v, shift), preferred_element_type=F32
                ).astype(BF16)
        for v in range(nvec):
            acc[slot, v] = lax.dot_general(
                mid[v], rcat[...], (((1,), (1,)), ((), ())), preferred_element_type=F32
            ).reshape(4, 2, blk // 8, blk)

    def level0(t):
        return pltpu.make_async_remote_copy(
            src_ref=s0.at[t], dst_ref=r0.at[t], send_sem=send0.at[t], recv_sem=recv0.at[t],
            device_id=sibling, device_id_type=MESH,
        )

    def level1(t):
        return pltpu.make_async_remote_copy(
            src_ref=s1.at[t, e], dst_ref=r1.at[t], send_sem=send1.at[t], recv_sem=recv1.at[t],
            device_id=partner, device_id_type=MESH,
        )

    def level2(t, p):
        return pltpu.make_async_remote_copy(
            src_ref=s2.at[t, p - 1], dst_ref=r2.at[p - 1, t],
            send_sem=send2.at[t, p - 1], recv_sem=recv2.at[t, p - 1],
            device_id=at(z + jnp.where(e == 1, p, -p), yx), device_id_type=MESH,
        )

    def stage0(t, slot):
        s0[t] = acc[slot, :, :, other].astype(BF16)
        level0(t).start()

    def stage1(t, slot):
        level0(t).wait_recv()
        for zl2 in range(4):
            for zh2 in range(2):
                lanes = slice(zh2 * half, (zh2 + 1) * half)
                value = acc[slot, :, zl2, core, :, lanes] + r0[t, :, zl2, :, lanes].astype(F32)
                delta = lax.rem(zh2 * 4 + zl2 - (z - e) + 16, 8)
                low = (delta >= 1) & (delta <= 4)
                side = jnp.where(low, 0, 1)
                place = jnp.where(low, delta - 1, lax.rem(8 - delta, 8))
                s1[t, side, place] = value.astype(BF16)
                keep[t, side, place] = value
        level1(t).start()

    def stage2(t):
        level1(t).wait_recv()
        for p in range(4):
            value = keep[t, 1 - e, p] + r1[t, p].astype(F32)
            if p == 0:
                own[t] = value
            else:
                s2[t, p - 1] = value.astype(BF16)
                level2(t, p).start()

    inner = sectors - 2
    gap = LAG - 2
    def first():
        load_psi.wait()
        for copy in load_ops(1):
            copy.wait()
        compute(1, 0, lambda v, shift: psi[v, 1 - shift])

    if EARLY:
        first()
    pl.semaphore_wait(barrier, 4 + 7 + nyx - 1)
    for zl_from, side in ((3, 0), (0, 1)):
        @pl.when(zl == zl_from)
        def _():
            for hop, to_side in ((0, side), (1, side), (2, 1 - side)):
                for v in range(nvec):
                    source = psi_hbm.at[v, 0 if to_side else sectors - 1, mine]
                    halo(to_side, v, hop, source).start()

    if not EARLY:
        first()
    stage0(0, 0)

    @pl.loop(1, sectors + LAG)
    def _(m):
        @pl.when(m < inner)
        def _():
            t = sector_of(m)
            for copy in load_ops(t):
                copy.wait()
            compute(t, lax.rem(m, 2), lambda v, shift: psi[v, t - shift])
            stage0(m, lax.rem(m, 2))

        @pl.when(m == inner + gap)
        def _():
            for copy in edge_loads:
                copy.wait()
            for side in range(2):
                share(side).wait_recv()

        @pl.when((m >= inner + gap) & (m < sectors + gap))
        def _():
            n = m - gap
            t = sector_of(n)
            for copy in load_ops(t):
                copy.wait()
            which = n - inner
            compute(t, lax.rem(n, 2), lambda v, shift: edge[which, v, 1 - shift])
            stage0(n, lax.rem(n, 2))

        @pl.when(m <= inner)
        def _():
            stage1(m - 1, lax.rem(m - 1, 2))

        @pl.when((m > inner + gap) & (m <= sectors + gap))
        def _():
            n = m - 1 - gap
            stage1(n, lax.rem(n, 2))

        @pl.when((m >= RELAY) & (m < RELAY + nvec) & ((zl == 1) | (zl == 2)))
        def _():
            v = m - RELAY
            halo_in(role, v).wait_recv()
            halo(role, v, 0, edge.at[role, v, 2 * role, mine]).start()

            @pl.when(v == nvec - 1)
            def _():
                share(role).start()

        @pl.when(m >= LAG)
        def _():
            stage2(m - LAG)

        @pl.when(m == inner + gap - 1)
        def _():
            for side in range(2):
                @pl.when((zl == 0) | (zl == 3) | (role != side))
                def _():
                    for v in range(nvec):
                        halo_in(side, v).wait_recv()
                    share(side).start()

    near = jnp.where(lax.rem(e + lax.div(zl, 2), 2) == 1, 0, 1)
    part = blk // 8

    def spread(batch, d):
        far = lax.rem(yx + d, nyx)
        return pltpu.make_async_remote_copy(
            src_ref=wsend.at[batch, far], dst_ref=wrecv.at[batch, yx],
            send_sem=send3.at[batch, d], recv_sem=recv3.at[batch, d],
            device_id=at(z, far), device_id_type=MESH,
        )

    def keep_own(batch):
        return pltpu.make_async_copy(
            wsend.at[batch, yx], wrecv.at[batch, yx], self_sem.at[batch]
        )

    for batch in range(2):
        ns = slice(batch * 4, batch * 4 + 4)

        @pl.loop(batch * 4, batch * 4 + 4)
        def _(n):
            for p in range(1, 4):
                level2(n, p).wait_recv()

        @pl.loop(0, nvec)
        def _(v):
            for group in range(2):
                if group == 0:
                    value = own[ns, v] + r2[near, ns, v].astype(F32)
                else:
                    value = r2[1 - near, ns, v].astype(F32) + r2[2, ns, v].astype(F32)
                turn[group] = value.reshape(4 * part, half).T
                for lq in range(2):
                    pieces = [turn[group, pl.ds(lq * 4 + r, nyx, stride=8), :] for r in range(4)]
                    for n4 in range(4):
                        lanes = slice(n4 * part, (n4 + 1) * part)
                        joined = jnp.concatenate([piece[:, lanes] for piece in pieces], axis=1)
                        wide[batch, v * 2 + lq, pl.ds(group * 4 + n4, nyx, stride=8), :] = joined

        for tile in range(6):
            lanes = slice(tile * 128, (tile + 1) * 128)
            wsend[batch, :, :, lanes] = wide[batch, tile].reshape(nyx, 8, 128).astype(BF16)

        @pl.loop(1, nyx)
        def _(d):
            spread(batch, d).start()

        keep_own(batch).start()

    for batch in range(2):
        keep_own(batch).wait()

        @pl.loop(1, nyx)
        def _(d):
            spread(batch, d).wait_recv()

        for tile in range(6):
            lanes = slice(tile * 128, (tile + 1) * 128)
            value = wrecv[batch, :, :, lanes].astype(F32).reshape(128, 128)
            flat[lanes, batch * 128 : (batch + 1) * 128] = value.T.astype(BF16)

    for v in range(nvec):
        rows = slice(v * blk, (v + 1) * blk)
        out_ref[rows] = jnp.dot(
            flat[rows], order[...], preferred_element_type=F32
        ).astype(BF16)

    for v in range(nvec):
        halo(role, v, 0, edge.at[role, v, 2 * role, mine]).wait_send()

    @pl.when((zl == 0) | (zl == 3))
    def _():
        for hop in (1, 2):
            for v in range(nvec):
                halo(role, v, hop, edge.at[role, v, 2 * role, mine]).wait_send()

    for side in range(2):
        share(side).wait_send()

    @pl.loop(0, sectors)
    def _(n):
        level0(n).wait_send()
        level1(n).wait_send()
        for p in range(1, 4):
            level2(n, p).wait_send()

    for batch in range(2):
        @pl.loop(1, nyx)
        def _(d):
            spread(batch, d).wait_send()


def solution(mesh):
    nsec = mesh.shape["sec"]
    nyx = nsec // 2

    def per_device(psi, left_ops, right_ops, shifts, active):
        nvec, sectors, blk = psi.shape[:3]
        count = left_ops.shape[0]
        part, half = blk // 8, blk // 2
        sizes = (nyx, count, nvec, sectors, blk)
        smem = pl.BlockSpec(memory_space=pltpu.SMEM)
        hbm = pl.BlockSpec(memory_space=pl.ANY)
        dma = pltpu.SemaphoreType.DMA
        result = pl.pallas_call(
            functools.partial(kernel, nsec * sectors, sizes),
            out_shape=jax.ShapeDtypeStruct((nvec * blk, blk), BF16),
            in_specs=[smem, smem, hbm, hbm, hbm],
            out_specs=pl.BlockSpec(memory_space=pltpu.VMEM),
            scratch_shapes=[
                pltpu.VMEM((nvec, sectors, blk, blk), BF16),
                pltpu.VMEM((2, nvec, 3, blk, blk), BF16),
                pltpu.VMEM((sectors, count, blk, blk), BF16),
                pltpu.VMEM((sectors, count, blk, blk), BF16),
                pltpu.VMEM((blk, blk), BF16),
                pltpu.VMEM((nvec, blk, count * blk), BF16),
                pltpu.VMEM((blk, count * blk), BF16),
                pltpu.VMEM((2, nvec, 4, 2, part, blk), F32),
                pltpu.VMEM((sectors, nvec, 4, part, blk), BF16),
                pltpu.VMEM((sectors, nvec, 4, part, blk), BF16),
                pltpu.VMEM((sectors, 2, 4, nvec, part, half), BF16),
                pltpu.VMEM((sectors, 2, 4, nvec, part, half), F32),
                pltpu.VMEM((sectors, 4, nvec, part, half), BF16),
                pltpu.VMEM((sectors, 3, nvec, part, half), BF16),
                pltpu.VMEM((sectors, nvec, part, half), F32),
                pltpu.VMEM((3, sectors, nvec, part, half), BF16),
                pltpu.VMEM((2, 128, 128), F32),
                pltpu.VMEM((2, nvec * 2, nyx * 8, 128), F32),
                pltpu.VMEM((2, nyx, 8, nvec * blk), BF16),
                pltpu.VMEM((2, nyx, 8, nvec * blk), BF16),
                pltpu.VMEM((blk, blk), BF16),
                pltpu.VMEM((nvec * blk, blk), BF16),
                dma,
                dma((2, sectors)),
                dma((2,)),
                dma((3, nvec)), dma((2, nvec)), dma((2,)), dma((2,)),
                dma((sectors,)), dma((sectors,)), dma((sectors,)), dma((sectors,)),
                dma((sectors, 3)), dma((sectors, 3)),
                dma((2, nyx)), dma((2, nyx)),
                dma((2,)),
            ],
            compiler_params=pltpu.CompilerParams(
                collective_id=0, has_side_effects=True, vmem_limit_bytes=56 * 1024 * 1024
            ),
        )(shifts, active, psi, left_ops, right_ops)
        return result.reshape(nvec, blk // nsec, blk // 8, blk).transpose(0, 1, 3, 2)

    return jax.shard_map(
        per_device,
        mesh=mesh,
        in_specs=(
            P(None, "sec", None, None),
            P("op", "sec", None, None),
            P("op", "sec", None, None),
            P("op"),
            P("op", "sec"),
        ),
        out_specs=P(None, "sec", None, "op"),
        check_vma=False,
    )
```

```python
import functools

import jax
import jax.numpy as jnp
from jax import lax
from jax.experimental import pallas as pl
from jax.experimental.pallas import tpu as pltpu
from jax.sharding import PartitionSpec as P

MESH = pl.DeviceIdType.MESH
F32 = jnp.float32
BF16 = jnp.bfloat16
LAG = 4
RELAY = 2
EARLY = False


def kernel(
    nsec_total, sizes, shifts, active, psi_hbm, left_hbm, right_hbm, wrecv,
    psi, edge, left, right, perm, mid, rcat, acc,
    s0, r0, s1, keep, r1, s2, own, r2, turn, wide, wsend,
    load_sem, op_sem, edge_sem, halo_send, halo_recv, sib_send, sib_recv,
    send0, recv0, send1, recv1, send2, recv2, send3, recv3, self_sem,
):
    nyx, count, nvec, sectors, blk = sizes
    assert (nyx, sectors, blk) == (16, 8, 256)
    op, sec = lax.axis_index("op"), lax.axis_index("sec")
    zl, core = lax.div(op, 2), lax.rem(op, 2)
    yx, zh = lax.div(sec, 2), lax.rem(sec, 2)
    z = zh * 4 + zl
    e = lax.rem(zl, 2)
    other = 1 - core
    nsec = 2 * nyx
    half = blk // 2

    def at(zz, yxx):
        zz = lax.rem(zz + 16, 8)
        return {"op": lax.rem(zz, 4) * 2 + core, "sec": yxx * 2 + lax.div(zz, 4)}

    sibling = {"op": zl * 2 + other, "sec": sec}
    partner = at(z + 1 - 2 * e, yx)
    sec_up, sec_down = lax.rem(sec + 1, nsec), lax.rem(sec + nsec - 1, nsec)

    def chain(zls, secs):
        pick = lambda w: jnp.where(zl == 0, w[0], jnp.where(zl == 1, w[1], jnp.where(zl == 2, w[2], w[3])))
        return {"op": pick(zls) * 2 + core, "sec": pick(secs)}

    halo_to = (
        chain((2, 2, 1, 1), (sec_down, sec, sec, sec_up)),
        chain((3, 3, 0, 0), (sec_down, sec, sec, sec_up)),
        chain((3, 3, 0, 0), (sec_up, sec, sec, sec_down)),
    )
    greets = (
        chain((2, 3, 0, 1), (sec_down, sec_down, sec_up, sec_up)),
        chain((3, 2, 1, 0), (sec_down, sec, sec, sec_up)),
        chain((3, 2, 1, 0), (sec_up, sec, sec, sec_down)),
    )

    barrier = pltpu.get_barrier_semaphore()
    pl.semaphore_signal(barrier, inc=1, device_id=sibling, device_id_type=MESH)
    for peer in greets:
        pl.semaphore_signal(barrier, inc=1, device_id=peer, device_id_type=MESH)

    @pl.loop(1, 8)
    def _(d):
        pl.semaphore_signal(barrier, inc=1, device_id=at(z + d, yx), device_id_type=MESH)

    @pl.loop(1, nyx)
    def _(d):
        pl.semaphore_signal(
            barrier, inc=1, device_id=at(z, lax.rem(yx + d, nyx)), device_id_type=MESH
        )

    load_psi = pltpu.make_async_copy(psi_hbm, psi, load_sem)

    def sector_of(n):
        return jnp.where(n < sectors - 2, n + 1, jnp.where(n == sectors - 2, 0, sectors - 1))

    def load_ops(t):
        return (
            pltpu.make_async_copy(left_hbm.at[:, t], left.at[t], op_sem.at[0, t]),
            pltpu.make_async_copy(right_hbm.at[:, t], right.at[t], op_sem.at[1, t]),
        )

    for copy in load_ops(1):
        copy.start()
    load_psi.start()

    @pl.loop(1, sectors)
    def _(n):
        for copy in load_ops(sector_of(n)):
            copy.start()

    edge_loads = (
        pltpu.make_async_copy(psi_hbm.at[:, 0:2], edge.at[0, :, 1:3], edge_sem.at[0]),
        pltpu.make_async_copy(
            psi_hbm.at[:, sectors - 2 : sectors], edge.at[1, :, 0:2], edge_sem.at[1]
        ),
    )
    for copy in edge_loads:
        copy.start()

    row = lax.broadcasted_iota(jnp.int32, (blk, blk), 0)
    col = lax.broadcasted_iota(jnp.int32, (blk, blk), 1)
    want = ((row & 120) << 1) | ((row & 128) >> 4) | (row & 7)
    perm[...] = jnp.where(col == want, 1.0, 0.0).astype(BF16)

    mine = pl.ds(core * half, half)
    role = 1 - e

    def halo(side, v, hop, source):
        return pltpu.make_async_remote_copy(
            src_ref=source,
            dst_ref=edge.at[side, v, 2 * side, mine],
            send_sem=halo_send.at[hop, v],
            recv_sem=halo_recv.at[side, v],
            device_id=halo_to[hop],
            device_id_type=MESH,
        )

    def halo_in(side, v):
        return pltpu.make_async_remote_copy(
            src_ref=edge.at[side, v, 2 * side, mine],
            dst_ref=edge.at[side, v, 2 * side, mine],
            send_sem=halo_send.at[0, v],
            recv_sem=halo_recv.at[side, v],
            device_id=sibling,
            device_id_type=MESH,
        )

    def share(side):
        return pltpu.make_async_remote_copy(
            src_ref=edge.at[side, :, 2 * side, mine],
            dst_ref=edge.at[side, :, 2 * side, mine],
            send_sem=sib_send.at[side],
            recv_sem=sib_recv.at[side],
            device_id=sibling,
            device_id_type=MESH,
        )

    def compute(t, slot, source):
        for k in range(count):
            shift = shifts[k]
            anchor = sec * sectors + t - shift
            good = (anchor >= 0) & (anchor < nsec_total)
            weight = jnp.where(good, active[k, t], 0).astype(F32)
            moved = jnp.dot(perm[...], right[t, k], preferred_element_type=F32)
            rcat[:, k * blk : (k + 1) * blk] = (moved * weight).astype(BF16)
            for v in range(nvec):
                mid[v, :, k * blk : (k + 1) * blk] = jnp.dot(
                    left[t, k], source(v, shift), preferred_element_type=F32
                ).astype(BF16)
        for v in range(nvec):
            acc[slot, v] = lax.dot_general(
                mid[v], rcat[...], (((1,), (1,)), ((), ())), preferred_element_type=F32
            ).reshape(4, 2, blk // 8, blk)

    def level0(t):
        return pltpu.make_async_remote_copy(
            src_ref=s0.at[t], dst_ref=r0.at[t], send_sem=send0.at[t], recv_sem=recv0.at[t],
            device_id=sibling, device_id_type=MESH,
        )

    def level1(t):
        return pltpu.make_async_remote_copy(
            src_ref=s1.at[t, e], dst_ref=r1.at[t], send_sem=send1.at[t], recv_sem=recv1.at[t],
            device_id=partner, device_id_type=MESH,
        )

    def level2(t, p):
        return pltpu.make_async_remote_copy(
            src_ref=s2.at[t, p - 1], dst_ref=r2.at[p - 1, t],
            send_sem=send2.at[t, p - 1], recv_sem=recv2.at[t, p - 1],
            device_id=at(z + jnp.where(e == 1, p, -p), yx), device_id_type=MESH,
        )

    def stage0(t, slot):
        s0[t] = acc[slot, :, :, other].astype(BF16)
        level0(t).start()

    def stage1(t, slot):
        level0(t).wait_recv()
        for zl2 in range(4):
            for zh2 in range(2):
                lanes = slice(zh2 * half, (zh2 + 1) * half)
                value = acc[slot, :, zl2, core, :, lanes] + r0[t, :, zl2, :, lanes].astype(F32)
                delta = lax.rem(zh2 * 4 + zl2 - (z - e) + 16, 8)
                low = (delta >= 1) & (delta <= 4)
                side = jnp.where(low, 0, 1)
                place = jnp.where(low, delta - 1, lax.rem(8 - delta, 8))
                s1[t, side, place] = value.astype(BF16)
                keep[t, side, place] = value
        level1(t).start()

    def stage2(t):
        level1(t).wait_recv()
        for p in (3, 2, 1, 0):
            value = keep[t, 1 - e, p] + r1[t, p].astype(F32)
            if p == 0:
                own[t] = value
            else:
                s2[t, p - 1] = value.astype(BF16)
                level2(t, p).start()

    inner = sectors - 2
    gap = LAG - 2
    def first():
        load_psi.wait()
        for copy in load_ops(1):
            copy.wait()
        compute(1, 0, lambda v, shift: psi[v, 1 - shift])

    if EARLY:
        first()
    pl.semaphore_wait(barrier, 4 + 7 + nyx - 1)
    for zl_from, side in ((3, 0), (0, 1)):
        @pl.when(zl == zl_from)
        def _():
            for hop, to_side in ((0, side), (1, side), (2, 1 - side)):
                for v in range(nvec):
                    source = psi_hbm.at[v, 0 if to_side else sectors - 1, mine]
                    halo(to_side, v, hop, source).start()

    if not EARLY:
        first()
    stage0(0, 0)

    @pl.loop(1, sectors + LAG)
    def _(m):
        @pl.when(m < inner)
        def _():
            t = sector_of(m)
            for copy in load_ops(t):
                copy.wait()
            compute(t, lax.rem(m, 2), lambda v, shift: psi[v, t - shift])
            stage1(m - 1, lax.rem(m - 1, 2))
            stage0(m, lax.rem(m, 2))

        @pl.when(m == inner + gap)
        def _():
            for copy in edge_loads:
                copy.wait()
            for side in range(2):
                share(side).wait_recv()

        @pl.when((m >= inner + gap) & (m < sectors + gap))
        def _():
            n = m - gap
            t = sector_of(n)
            for copy in load_ops(t):
                copy.wait()
            which = n - inner
            compute(t, lax.rem(n, 2), lambda v, shift: edge[which, v, 1 - shift])
            stage0(n, lax.rem(n, 2))

        @pl.when(m == inner)
        def _():
            stage1(m - 1, lax.rem(m - 1, 2))

        @pl.when((m > inner + gap) & (m <= sectors + gap))
        def _():
            n = m - 1 - gap
            stage1(n, lax.rem(n, 2))

        @pl.when((m >= RELAY) & (m < RELAY + nvec) & ((zl == 1) | (zl == 2)))
        def _():
            v = m - RELAY
            halo_in(role, v).wait_recv()
            halo(role, v, 0, edge.at[role, v, 2 * role, mine]).start()

            @pl.when(v == nvec - 1)
            def _():
                share(role).start()

        @pl.when(m >= LAG)
        def _():
            stage2(m - LAG)

        @pl.when(m == inner + gap - 1)
        def _():
            for side in range(2):
                @pl.when((zl == 0) | (zl == 3) | (role != side))
                def _():
                    for v in range(nvec):
                        halo_in(side, v).wait_recv()
                    share(side).start()

    near = jnp.where(lax.rem(e + lax.div(zl, 2), 2) == 1, 0, 1)
    part = blk // 8

    def spread(batch, d):
        y, x = lax.div(yx, 4), lax.rem(yx, 4)
        far = lax.rem(y + lax.div(d, 4), 4) * 4 + lax.rem(x + lax.rem(d, 4), 4)
        return pltpu.make_async_remote_copy(
            src_ref=wsend.at[batch, far], dst_ref=wrecv.at[batch, yx],
            send_sem=send3.at[batch, d], recv_sem=recv3.at[batch, d],
            device_id=at(z, far), device_id_type=MESH,
        )

    def keep_own(batch):
        return pltpu.make_async_copy(
            wsend.at[batch, yx], wrecv.at[batch, yx], self_sem.at[batch]
        )

    for batch in range(2):
        ns = slice(batch * 4, batch * 4 + 4)

        @pl.loop(batch * 4, batch * 4 + 4)
        def _(n):
            for p in range(1, 4):
                level2(n, p).wait_recv()

        @pl.loop(0, nvec)
        def _(v):
            for group in range(2):
                if group == 0:
                    value = own[ns, v] + r2[near, ns, v].astype(F32)
                else:
                    value = r2[1 - near, ns, v].astype(F32) + r2[2, ns, v].astype(F32)
                turn[group] = value.reshape(4 * part, half).T
                for lq in range(2):
                    pieces = [turn[group, pl.ds(lq * 4 + r, nyx, stride=8), :] for r in range(4)]
                    for n4 in range(4):
                        lanes = slice(n4 * part, (n4 + 1) * part)
                        joined = jnp.concatenate([piece[:, lanes] for piece in pieces], axis=1)
                        wide[batch, v * 2 + lq, pl.ds(group * 4 + n4, nyx, stride=8), :] = joined

        for tile in range(6):
            lanes = slice(tile * 128, (tile + 1) * 128)
            wsend[batch, :, :, lanes] = wide[batch, tile].reshape(nyx, 8, 128).astype(BF16)

        for d in sorted(range(1, nyx), key=lambda d: -(min(d // 4, 4 - d // 4) + min(d % 4, 4 - d % 4))):
            spread(batch, jnp.int32(d)).start()

        keep_own(batch).start()

    for batch in range(2):
        keep_own(batch).wait()

        @pl.loop(1, nyx)
        def _(d):
            spread(batch, d).wait_recv()

    for v in range(nvec):
        halo(role, v, 0, edge.at[role, v, 2 * role, mine]).wait_send()

    @pl.when((zl == 0) | (zl == 3))
    def _():
        for hop in (1, 2):
            for v in range(nvec):
                halo(role, v, hop, edge.at[role, v, 2 * role, mine]).wait_send()

    for side in range(2):
        share(side).wait_send()

    @pl.loop(0, sectors)
    def _(n):
        level0(n).wait_send()
        level1(n).wait_send()
        for p in range(1, 4):
            level2(n, p).wait_send()

    for batch in range(2):
        @pl.loop(1, nyx)
        def _(d):
            spread(batch, d).wait_send()


def transpose_kernel(rows_ref, out_ref, flat):
    zh = lax.rem(lax.axis_index("sec"), 2)
    blk = out_ref.shape[1]
    row = lax.broadcasted_iota(jnp.int32, (blk, blk), 0)
    col = lax.broadcasted_iota(jnp.int32, (blk, blk), 1)

    turn_n = ((row & 128) >> 5) | (row & 3)
    sector = jnp.where(turn_n < 6, turn_n + 1, jnp.where(turn_n == 6, 0, 7))
    group = jnp.where(zh == 1, 1 - ((row & 4) >> 2), (row & 4) >> 2)
    order = jnp.where(
        col == ((row & 120) << 1) + group * 8 + sector, 1.0, 0.0
    ).astype(BF16)
    for tile in range(out_ref.shape[0] // 128):
        lanes = slice(tile * 128, (tile + 1) * 128)
        for batch in range(2):
            value = rows_ref[batch, :, :, lanes].astype(F32).reshape(128, 128)
            flat[lanes, batch * 128 : (batch + 1) * 128] = value.T.astype(BF16)
    for start in range(0, out_ref.shape[0], blk):
        rows = slice(start, start + blk)
        out_ref[rows] = jnp.dot(flat[rows], order, preferred_element_type=F32).astype(BF16)


def solution(mesh):
    nsec = mesh.shape["sec"]
    nyx = nsec // 2

    def per_device(psi, left_ops, right_ops, shifts, active):
        nvec, sectors, blk = psi.shape[:3]
        count = left_ops.shape[0]
        part, half = blk // 8, blk // 2
        sizes = (nyx, count, nvec, sectors, blk)
        smem = pl.BlockSpec(memory_space=pltpu.SMEM)
        hbm = pl.BlockSpec(memory_space=pl.ANY)
        dma = pltpu.SemaphoreType.DMA
        result = pl.pallas_call(
            functools.partial(kernel, nsec * sectors, sizes),
            out_shape=jax.ShapeDtypeStruct((2, nyx, 8, nvec * blk), BF16),
            in_specs=[smem, smem, hbm, hbm, hbm],
            out_specs=hbm,
            scratch_shapes=[
                pltpu.VMEM((nvec, sectors, blk, blk), BF16),
                pltpu.VMEM((2, nvec, 3, blk, blk), BF16),
                pltpu.VMEM((sectors, count, blk, blk), BF16),
                pltpu.VMEM((sectors, count, blk, blk), BF16),
                pltpu.VMEM((blk, blk), BF16),
                pltpu.VMEM((nvec, blk, count * blk), BF16),
                pltpu.VMEM((blk, count * blk), BF16),
                pltpu.VMEM((2, nvec, 4, 2, part, blk), F32),
                pltpu.VMEM((sectors, nvec, 4, part, blk), BF16),
                pltpu.VMEM((sectors, nvec, 4, part, blk), BF16),
                pltpu.VMEM((sectors, 2, 4, nvec, part, half), BF16),
                pltpu.VMEM((sectors, 2, 4, nvec, part, half), F32),
                pltpu.VMEM((sectors, 4, nvec, part, half), BF16),
                pltpu.VMEM((sectors, 3, nvec, part, half), BF16),
                pltpu.VMEM((sectors, nvec, part, half), F32),
                pltpu.VMEM((3, sectors, nvec, part, half), BF16),
                pltpu.VMEM((2, 128, 128), F32),
                pltpu.VMEM((2, nvec * 2, nyx * 8, 128), F32),
                pltpu.VMEM((2, nyx, 8, nvec * blk), BF16),
                dma,
                dma((2, sectors)),
                dma((2,)),
                dma((3, nvec)), dma((2, nvec)), dma((2,)), dma((2,)),
                dma((sectors,)), dma((sectors,)), dma((sectors,)), dma((sectors,)),
                dma((sectors, 3)), dma((sectors, 3)),
                dma((2, nyx)), dma((2, nyx)),
                dma((2,)),
            ],
            compiler_params=pltpu.CompilerParams(
                collective_id=0, has_side_effects=True, vmem_limit_bytes=56 * 1024 * 1024
            ),
        )(shifts, active, psi, left_ops, right_ops)
        result = pl.pallas_call(
            transpose_kernel,
            out_shape=jax.ShapeDtypeStruct((nvec * blk, blk), BF16),
            in_specs=[pl.BlockSpec(memory_space=pltpu.VMEM)],
            out_specs=pl.BlockSpec(memory_space=pltpu.VMEM),
            scratch_shapes=[pltpu.VMEM((nvec * blk, blk), BF16)],
        )(result)
        return result.reshape(nvec, blk // nsec, blk // 8, blk).transpose(0, 1, 3, 2)

    return jax.shard_map(
        per_device,
        mesh=mesh,
        in_specs=(
            P(None, "sec", None, None),
            P("op", "sec", None, None),
            P("op", "sec", None, None),
            P("op"),
            P("op", "sec"),
        ),
        out_specs=P(None, "sec", None, "op"),
        check_vma=False,
    )
```

```python
import functools

import jax
import jax.numpy as jnp
from jax import lax
from jax.experimental import pallas as pl
from jax.experimental.pallas import tpu as pltpu
from jax.sharding import PartitionSpec as P

MESH = pl.DeviceIdType.MESH
F32 = jnp.float32
BF16 = jnp.bfloat16
LAG = 3
RELAY = 2
EARLY = False


def kernel(
    nsec_total, sizes, shifts, active, psi_hbm, left_hbm, right_hbm, wrecv,
    psi, edge, left, right, perm, mid, rcat, acc,
    s0, r0, s1, keep, r1, s2, own, r2, turn, wide, wsend,
    load_sem, op_sem, edge_sem, halo_send, halo_recv, sib_send, sib_recv,
    send0, recv0, send1, recv1, send2, recv2, send3, recv3, self_sem,
):
    nyx, count, nvec, sectors, blk = sizes
    assert (nyx, sectors, blk) == (16, 8, 256)
    op, sec = lax.axis_index("op"), lax.axis_index("sec")
    zl, core = lax.div(op, 2), lax.rem(op, 2)
    yx, zh = lax.div(sec, 2), lax.rem(sec, 2)
    z = zh * 4 + zl
    e = lax.rem(zl, 2)
    other = 1 - core
    nsec = 2 * nyx
    half = blk // 2

    def at(zz, yxx):
        zz = lax.rem(zz + 16, 8)
        return {"op": lax.rem(zz, 4) * 2 + core, "sec": yxx * 2 + lax.div(zz, 4)}

    sibling = {"op": zl * 2 + other, "sec": sec}
    partner = at(z + 1 - 2 * e, yx)
    sec_up, sec_down = lax.rem(sec + 1, nsec), lax.rem(sec + nsec - 1, nsec)

    def chain(zls, secs):
        pick = lambda w: jnp.where(zl == 0, w[0], jnp.where(zl == 1, w[1], jnp.where(zl == 2, w[2], w[3])))
        return {"op": pick(zls) * 2 + core, "sec": pick(secs)}

    halo_to = (
        chain((2, 2, 1, 1), (sec_down, sec, sec, sec_up)),
        chain((3, 3, 0, 0), (sec_down, sec, sec, sec_up)),
        chain((3, 3, 0, 0), (sec_up, sec, sec, sec_down)),
    )
    greets = (
        chain((2, 3, 0, 1), (sec_down, sec_down, sec_up, sec_up)),
        chain((3, 2, 1, 0), (sec_down, sec, sec, sec_up)),
        chain((3, 2, 1, 0), (sec_up, sec, sec, sec_down)),
    )

    barrier = pltpu.get_barrier_semaphore()
    pl.semaphore_signal(barrier, inc=1, device_id=sibling, device_id_type=MESH)
    for peer in greets:
        pl.semaphore_signal(barrier, inc=1, device_id=peer, device_id_type=MESH)

    @pl.loop(1, 8)
    def _(d):
        pl.semaphore_signal(barrier, inc=1, device_id=at(z + d, yx), device_id_type=MESH)

    @pl.loop(1, nyx)
    def _(d):
        pl.semaphore_signal(
            barrier, inc=1, device_id=at(z, lax.rem(yx + d, nyx)), device_id_type=MESH
        )

    load_psi = pltpu.make_async_copy(psi_hbm, psi, load_sem)

    def sector_of(n):
        return jnp.where(n < sectors - 2, n + 1, jnp.where(n == sectors - 2, 0, sectors - 1))

    def load_ops(t):
        return (
            pltpu.make_async_copy(left_hbm.at[:, t], left.at[t], op_sem.at[0, t]),
            pltpu.make_async_copy(right_hbm.at[:, t], right.at[t], op_sem.at[1, t]),
        )

    for copy in load_ops(1):
        copy.start()
    load_psi.start()

    @pl.loop(1, sectors)
    def _(n):
        for copy in load_ops(sector_of(n)):
            copy.start()

    edge_loads = (
        pltpu.make_async_copy(psi_hbm.at[:, 0:2], edge.at[0, :, 1:3], edge_sem.at[0]),
        pltpu.make_async_copy(
            psi_hbm.at[:, sectors - 2 : sectors], edge.at[1, :, 0:2], edge_sem.at[1]
        ),
    )
    for copy in edge_loads:
        copy.start()

    row = lax.broadcasted_iota(jnp.int32, (blk, blk), 0)
    col = lax.broadcasted_iota(jnp.int32, (blk, blk), 1)
    want = ((row & 120) << 1) | ((row & 128) >> 4) | (row & 7)
    perm[...] = jnp.where(col == want, 1.0, 0.0).astype(BF16)

    mine = pl.ds(core * half, half)
    role = 1 - e

    def halo(side, v, hop, source):
        return pltpu.make_async_remote_copy(
            src_ref=source,
            dst_ref=edge.at[side, v, 2 * side, mine],
            send_sem=halo_send.at[hop, v],
            recv_sem=halo_recv.at[side, v],
            device_id=halo_to[hop],
            device_id_type=MESH,
        )

    def halo_in(side, v):
        return pltpu.make_async_remote_copy(
            src_ref=edge.at[side, v, 2 * side, mine],
            dst_ref=edge.at[side, v, 2 * side, mine],
            send_sem=halo_send.at[0, v],
            recv_sem=halo_recv.at[side, v],
            device_id=sibling,
            device_id_type=MESH,
        )

    def share(side):
        return pltpu.make_async_remote_copy(
            src_ref=edge.at[side, :, 2 * side, mine],
            dst_ref=edge.at[side, :, 2 * side, mine],
            send_sem=sib_send.at[side],
            recv_sem=sib_recv.at[side],
            device_id=sibling,
            device_id_type=MESH,
        )

    def compute(t, slot, source):
        for k in range(count):
            shift = shifts[k]
            anchor = sec * sectors + t - shift
            good = (anchor >= 0) & (anchor < nsec_total)
            weight = jnp.where(good, active[k, t], 0).astype(F32)
            moved = jnp.dot(perm[...], right[t, k], preferred_element_type=F32)
            rcat[:, k * blk : (k + 1) * blk] = (moved * weight).astype(BF16)
            for v in range(nvec):
                mid[v, :, k * blk : (k + 1) * blk] = jnp.dot(
                    left[t, k], source(v, shift), preferred_element_type=F32
                ).astype(BF16)
        for v in range(nvec):
            acc[slot, v] = lax.dot_general(
                mid[v], rcat[...], (((1,), (1,)), ((), ())), preferred_element_type=F32
            ).reshape(4, 2, blk // 8, blk)

    def level0(t):
        return pltpu.make_async_remote_copy(
            src_ref=s0.at[t], dst_ref=r0.at[t], send_sem=send0.at[t], recv_sem=recv0.at[t],
            device_id=sibling, device_id_type=MESH,
        )

    def level1(t):
        return pltpu.make_async_remote_copy(
            src_ref=s1.at[t, e], dst_ref=r1.at[t], send_sem=send1.at[t], recv_sem=recv1.at[t],
            device_id=partner, device_id_type=MESH,
        )

    def level2(t, p):
        return pltpu.make_async_remote_copy(
            src_ref=s2.at[t, p - 1], dst_ref=r2.at[p - 1, t],
            send_sem=send2.at[t, p - 1], recv_sem=recv2.at[t, p - 1],
            device_id=at(z + jnp.where(e == 1, p, -p), yx), device_id_type=MESH,
        )

    def stage0(t, slot):
        s0[t] = acc[slot, :, :, other].astype(BF16)
        level0(t).start()

    def stage1(t, slot):
        level0(t).wait_recv()
        for zl2 in range(4):
            for zh2 in range(2):
                lanes = slice(zh2 * half, (zh2 + 1) * half)
                value = acc[slot, :, zl2, core, :, lanes] + r0[t, :, zl2, :, lanes].astype(F32)
                delta = lax.rem(zh2 * 4 + zl2 - (z - e) + 16, 8)
                low = (delta >= 1) & (delta <= 4)
                side = jnp.where(low, 0, 1)
                place = jnp.where(low, delta - 1, lax.rem(8 - delta, 8))
                s1[t, side, place] = value.astype(BF16)
                keep[t, side, place] = value
        level1(t).start()

    def stage2(t):
        level1(t).wait_recv()
        for p in (3, 2, 1, 0):
            value = keep[t, 1 - e, p] + r1[t, p].astype(F32)
            if p == 0:
                own[t] = value
            else:
                s2[t, p - 1] = value.astype(BF16)
                level2(t, p).start()

    inner = sectors - 2
    gap = LAG - 2
    def first():
        load_psi.wait()
        for copy in load_ops(1):
            copy.wait()
        compute(1, 0, lambda v, shift: psi[v, 1 - shift])

    if EARLY:
        first()
    pl.semaphore_wait(barrier, 4 + 7 + nyx - 1)
    for zl_from, side in ((3, 0), (0, 1)):
        @pl.when(zl == zl_from)
        def _():
            for hop, to_side in ((0, side), (1, side), (2, 1 - side)):
                for v in range(nvec):
                    source = psi_hbm.at[v, 0 if to_side else sectors - 1, mine]
                    halo(to_side, v, hop, source).start()

    if not EARLY:
        first()
    stage0(0, 0)

    @pl.loop(1, sectors + LAG)
    def _(m):
        @pl.when(m < inner)
        def _():
            t = sector_of(m)
            for copy in load_ops(t):
                copy.wait()
            compute(t, lax.rem(m, 2), lambda v, shift: psi[v, t - shift])
            stage1(m - 1, lax.rem(m - 1, 2))
            stage0(m, lax.rem(m, 2))

        @pl.when(m == inner + gap)
        def _():
            for copy in edge_loads:
                copy.wait()
            for side in range(2):
                share(side).wait_recv()

        @pl.when((m >= inner + gap) & (m < sectors + gap))
        def _():
            n = m - gap
            t = sector_of(n)
            for copy in load_ops(t):
                copy.wait()
            which = n - inner
            compute(t, lax.rem(n, 2), lambda v, shift: edge[which, v, 1 - shift])
            stage0(n, lax.rem(n, 2))

        @pl.when(m == inner)
        def _():
            stage1(m - 1, lax.rem(m - 1, 2))

        @pl.when((m > inner + gap) & (m <= sectors + gap))
        def _():
            n = m - 1 - gap
            stage1(n, lax.rem(n, 2))

        @pl.when((m >= RELAY) & (m < RELAY + nvec) & ((zl == 1) | (zl == 2)))
        def _():
            v = m - RELAY
            halo_in(role, v).wait_recv()
            halo(role, v, 0, edge.at[role, v, 2 * role, mine]).start()

            @pl.when(v == nvec - 1)
            def _():
                share(role).start()

        @pl.when(m >= LAG)
        def _():
            stage2(m - LAG)

        @pl.when(m == inner + gap - 1)
        def _():
            for side in range(2):
                @pl.when((zl == 0) | (zl == 3) | (role != side))
                def _():
                    for v in range(nvec):
                        halo_in(side, v).wait_recv()
                    share(side).start()

    near = jnp.where(lax.rem(e + lax.div(zl, 2), 2) == 1, 0, 1)
    part = blk // 8

    def spread(batch, d):
        y, x = lax.div(yx, 4), lax.rem(yx, 4)
        far = lax.rem(y + lax.div(d, 4), 4) * 4 + lax.rem(x + lax.rem(d, 4), 4)
        return pltpu.make_async_remote_copy(
            src_ref=wsend.at[batch, far], dst_ref=wrecv.at[batch, yx],
            send_sem=send3.at[batch, d], recv_sem=recv3.at[batch, d],
            device_id=at(z, far), device_id_type=MESH,
        )

    def keep_own(batch):
        return pltpu.make_async_copy(
            wsend.at[batch, yx], wrecv.at[batch, yx], self_sem.at[batch]
        )

    for batch in range(2):
        ns = slice(batch * 4, batch * 4 + 4)

        @pl.loop(batch * 4, batch * 4 + 4)
        def _(n):
            for p in range(1, 4):
                level2(n, p).wait_recv()

        @pl.loop(0, nvec)
        def _(v):
            for group in range(2):
                if group == 0:
                    value = own[ns, v] + r2[near, ns, v].astype(F32)
                else:
                    value = r2[1 - near, ns, v].astype(F32) + r2[2, ns, v].astype(F32)
                turn[group] = value.reshape(4 * part, half).T
                for lq in range(2):
                    pieces = [turn[group, pl.ds(lq * 4 + r, nyx, stride=8), :] for r in range(4)]
                    for n4 in range(4):
                        lanes = slice(n4 * part, (n4 + 1) * part)
                        joined = jnp.concatenate([piece[:, lanes] for piece in pieces], axis=1)
                        wide[batch, v * 2 + lq, pl.ds(group * 4 + n4, nyx, stride=8), :] = joined

        for tile in range(6):
            lanes = slice(tile * 128, (tile + 1) * 128)
            wsend[batch, :, :, lanes] = wide[batch, tile].reshape(nyx, 8, 128).astype(BF16)

        for d in sorted(range(1, nyx), key=lambda d: -(min(d // 4, 4 - d // 4) + min(d % 4, 4 - d % 4))):
            spread(batch, jnp.int32(d)).start()

        keep_own(batch).start()

    for batch in range(2):
        keep_own(batch).wait()

        @pl.loop(1, nyx)
        def _(d):
            spread(batch, d).wait_recv()

    for v in range(nvec):
        halo(role, v, 0, edge.at[role, v, 2 * role, mine]).wait_send()

    @pl.when((zl == 0) | (zl == 3))
    def _():
        for hop in (1, 2):
            for v in range(nvec):
                halo(role, v, hop, edge.at[role, v, 2 * role, mine]).wait_send()

    for side in range(2):
        share(side).wait_send()

    @pl.loop(0, sectors)
    def _(n):
        level0(n).wait_send()
        level1(n).wait_send()
        for p in range(1, 4):
            level2(n, p).wait_send()

    for batch in range(2):
        @pl.loop(1, nyx)
        def _(d):
            spread(batch, d).wait_send()


def transpose_kernel(rows_ref, out_ref, flat):
    zh = lax.rem(lax.axis_index("sec"), 2)
    blk = out_ref.shape[1]
    row = lax.broadcasted_iota(jnp.int32, (blk, blk), 0)
    col = lax.broadcasted_iota(jnp.int32, (blk, blk), 1)

    turn_n = ((row & 128) >> 5) | (row & 3)
    sector = jnp.where(turn_n < 6, turn_n + 1, jnp.where(turn_n == 6, 0, 7))
    group = jnp.where(zh == 1, 1 - ((row & 4) >> 2), (row & 4) >> 2)
    order = jnp.where(
        col == ((row & 120) << 1) + group * 8 + sector, 1.0, 0.0
    ).astype(BF16)
    for tile in range(out_ref.shape[0] // 128):
        lanes = slice(tile * 128, (tile + 1) * 128)
        for batch in range(2):
            value = rows_ref[batch, :, :, lanes].astype(F32).reshape(128, 128)
            flat[lanes, batch * 128 : (batch + 1) * 128] = value.T.astype(BF16)
    for start in range(0, out_ref.shape[0], blk):
        rows = slice(start, start + blk)
        out_ref[rows] = jnp.dot(flat[rows], order, preferred_element_type=F32).astype(BF16)


def solution(mesh):
    nsec = mesh.shape["sec"]
    nyx = nsec // 2

    def per_device(psi, left_ops, right_ops, shifts, active):
        nvec, sectors, blk = psi.shape[:3]
        count = left_ops.shape[0]
        part, half = blk // 8, blk // 2
        sizes = (nyx, count, nvec, sectors, blk)
        smem = pl.BlockSpec(memory_space=pltpu.SMEM)
        hbm = pl.BlockSpec(memory_space=pl.ANY)
        dma = pltpu.SemaphoreType.DMA
        result = pl.pallas_call(
            functools.partial(kernel, nsec * sectors, sizes),
            out_shape=jax.ShapeDtypeStruct((2, nyx, 8, nvec * blk), BF16),
            in_specs=[smem, smem, hbm, hbm, hbm],
            out_specs=hbm,
            scratch_shapes=[
                pltpu.VMEM((nvec, sectors, blk, blk), BF16),
                pltpu.VMEM((2, nvec, 3, blk, blk), BF16),
                pltpu.VMEM((sectors, count, blk, blk), BF16),
                pltpu.VMEM((sectors, count, blk, blk), BF16),
                pltpu.VMEM((blk, blk), BF16),
                pltpu.VMEM((nvec, blk, count * blk), BF16),
                pltpu.VMEM((blk, count * blk), BF16),
                pltpu.VMEM((2, nvec, 4, 2, part, blk), F32),
                pltpu.VMEM((sectors, nvec, 4, part, blk), BF16),
                pltpu.VMEM((sectors, nvec, 4, part, blk), BF16),
                pltpu.VMEM((sectors, 2, 4, nvec, part, half), BF16),
                pltpu.VMEM((sectors, 2, 4, nvec, part, half), F32),
                pltpu.VMEM((sectors, 4, nvec, part, half), BF16),
                pltpu.VMEM((sectors, 3, nvec, part, half), BF16),
                pltpu.VMEM((sectors, nvec, part, half), F32),
                pltpu.VMEM((3, sectors, nvec, part, half), BF16),
                pltpu.VMEM((2, 128, 128), F32),
                pltpu.VMEM((2, nvec * 2, nyx * 8, 128), F32),
                pltpu.VMEM((2, nyx, 8, nvec * blk), BF16),
                dma,
                dma((2, sectors)),
                dma((2,)),
                dma((3, nvec)), dma((2, nvec)), dma((2,)), dma((2,)),
                dma((sectors,)), dma((sectors,)), dma((sectors,)), dma((sectors,)),
                dma((sectors, 3)), dma((sectors, 3)),
                dma((2, nyx)), dma((2, nyx)),
                dma((2,)),
            ],
            compiler_params=pltpu.CompilerParams(
                collective_id=0, has_side_effects=True, vmem_limit_bytes=56 * 1024 * 1024
            ),
        )(shifts, active, psi, left_ops, right_ops)
        result = pl.pallas_call(
            transpose_kernel,
            out_shape=jax.ShapeDtypeStruct((nvec * blk, blk), BF16),
            in_specs=[pl.BlockSpec(memory_space=pltpu.VMEM)],
            out_specs=pl.BlockSpec(memory_space=pltpu.VMEM),
            scratch_shapes=[pltpu.VMEM((nvec * blk, blk), BF16)],
        )(result)
        return result.reshape(nvec, blk // nsec, blk // 8, blk).transpose(0, 1, 3, 2)

    return jax.shard_map(
        per_device,
        mesh=mesh,
        in_specs=(
            P(None, "sec", None, None),
            P("op", "sec", None, None),
            P("op", "sec", None, None),
            P("op"),
            P("op", "sec"),
        ),
        out_specs=P(None, "sec", None, "op"),
        check_vma=False,
    )
```

```python
import functools

import jax
import jax.numpy as jnp
from jax import lax
from jax.experimental import pallas as pl
from jax.experimental.pallas import tpu as pltpu
from jax.sharding import PartitionSpec as P

MESH = pl.DeviceIdType.MESH
F32 = jnp.float32
BF16 = jnp.bfloat16
LAG = 3
RELAY = 2
EARLY = False


def kernel(
    nsec_total, sizes, shifts, active, psi_hbm, left_hbm, right_hbm, wrecv,
    psi, edge, left, right, perm, mid, rcat, acc,
    s0, r0, s1, keep, r1, s2, own, r2, turn, wide, wsend,
    load_sem, op_sem, edge_sem, halo_send, halo_recv, sib_send, sib_recv,
    send0, recv0, send1, recv1, send2, recv2, send3, recv3, self_sem,
):
    nyx, count, nvec, sectors, blk = sizes
    assert (nyx, sectors, blk) == (16, 8, 256)
    op, sec = lax.axis_index("op"), lax.axis_index("sec")
    zl, core = lax.div(op, 2), lax.rem(op, 2)
    yx, zh = lax.div(sec, 2), lax.rem(sec, 2)
    z = zh * 4 + zl
    e = lax.rem(zl, 2)
    other = 1 - core
    nsec = 2 * nyx
    half = blk // 2

    def at(zz, yxx):
        zz = lax.rem(zz + 16, 8)
        return {"op": lax.rem(zz, 4) * 2 + core, "sec": yxx * 2 + lax.div(zz, 4)}

    sibling = {"op": zl * 2 + other, "sec": sec}
    partner = at(z + 1 - 2 * e, yx)
    sec_up, sec_down = lax.rem(sec + 1, nsec), lax.rem(sec + nsec - 1, nsec)

    def chain(zls, secs):
        pick = lambda w: jnp.where(zl == 0, w[0], jnp.where(zl == 1, w[1], jnp.where(zl == 2, w[2], w[3])))
        return {"op": pick(zls) * 2 + core, "sec": pick(secs)}

    halo_to = (
        chain((2, 2, 1, 1), (sec_down, sec, sec, sec_up)),
        chain((3, 3, 0, 0), (sec_down, sec, sec, sec_up)),
        chain((3, 3, 0, 0), (sec_up, sec, sec, sec_down)),
    )
    greets = (
        chain((2, 3, 0, 1), (sec_down, sec_down, sec_up, sec_up)),
        chain((3, 2, 1, 0), (sec_down, sec, sec, sec_up)),
        chain((3, 2, 1, 0), (sec_up, sec, sec, sec_down)),
    )

    barrier = pltpu.get_barrier_semaphore()
    pl.semaphore_signal(barrier, inc=1, device_id=sibling, device_id_type=MESH)
    for peer in greets:
        pl.semaphore_signal(barrier, inc=1, device_id=peer, device_id_type=MESH)

    @pl.loop(1, 8)
    def _(d):
        pl.semaphore_signal(barrier, inc=1, device_id=at(z + d, yx), device_id_type=MESH)

    @pl.loop(1, nyx)
    def _(d):
        pl.semaphore_signal(
            barrier, inc=1, device_id=at(z, lax.rem(yx + d, nyx)), device_id_type=MESH
        )

    load_psi = pltpu.make_async_copy(psi_hbm, psi, load_sem)

    def sector_of(n):
        return jnp.where(n < sectors - 2, n + 1, jnp.where(n == sectors - 2, 0, sectors - 1))

    def load_ops(t):
        return (
            pltpu.make_async_copy(left_hbm.at[:, t], left.at[t], op_sem.at[0, t]),
            pltpu.make_async_copy(right_hbm.at[:, t], right.at[t], op_sem.at[1, t]),
        )

    for copy in load_ops(1):
        copy.start()
    load_psi.start()

    @pl.loop(1, sectors)
    def _(n):
        for copy in load_ops(sector_of(n)):
            copy.start()

    edge_loads = (
        pltpu.make_async_copy(psi_hbm.at[:, 0:2], edge.at[0, :, 1:3], edge_sem.at[0]),
        pltpu.make_async_copy(
            psi_hbm.at[:, sectors - 2 : sectors], edge.at[1, :, 0:2], edge_sem.at[1]
        ),
    )
    for copy in edge_loads:
        copy.start()

    row = lax.broadcasted_iota(jnp.int32, (blk, blk), 0)
    col = lax.broadcasted_iota(jnp.int32, (blk, blk), 1)
    want = ((row & 120) << 1) | ((row & 128) >> 4) | (row & 7)
    perm[...] = jnp.where(col == want, 1.0, 0.0).astype(BF16)

    mine = pl.ds(core * half, half)
    role = 1 - e

    def halo(side, v, hop, source):
        return pltpu.make_async_remote_copy(
            src_ref=source,
            dst_ref=edge.at[side, v, 2 * side, mine],
            send_sem=halo_send.at[hop, v],
            recv_sem=halo_recv.at[side, v],
            device_id=halo_to[hop],
            device_id_type=MESH,
        )

    def halo_in(side, v):
        return pltpu.make_async_remote_copy(
            src_ref=edge.at[side, v, 2 * side, mine],
            dst_ref=edge.at[side, v, 2 * side, mine],
            send_sem=halo_send.at[0, v],
            recv_sem=halo_recv.at[side, v],
            device_id=sibling,
            device_id_type=MESH,
        )

    def share(side):
        return pltpu.make_async_remote_copy(
            src_ref=edge.at[side, :, 2 * side, mine],
            dst_ref=edge.at[side, :, 2 * side, mine],
            send_sem=sib_send.at[side],
            recv_sem=sib_recv.at[side],
            device_id=sibling,
            device_id_type=MESH,
        )

    def compute(t, slot, source):
        for k in range(count):
            shift = shifts[k]
            anchor = sec * sectors + t - shift
            good = (anchor >= 0) & (anchor < nsec_total)
            weight = jnp.where(good, active[k, t], 0).astype(F32)
            moved = jnp.dot(perm[...], right[t, k], preferred_element_type=F32)
            rcat[:, k * blk : (k + 1) * blk] = (moved * weight).astype(BF16)
            for v in range(nvec):
                mid[v, :, k * blk : (k + 1) * blk] = jnp.dot(
                    left[t, k], source(v, shift), preferred_element_type=F32
                ).astype(BF16)
        for v in range(nvec):
            acc[slot, v] = lax.dot_general(
                mid[v], rcat[...], (((1,), (1,)), ((), ())), preferred_element_type=F32
            ).reshape(4, 2, blk // 8, blk)

    def level0(t):
        return pltpu.make_async_remote_copy(
            src_ref=s0.at[t], dst_ref=r0.at[t], send_sem=send0.at[t], recv_sem=recv0.at[t],
            device_id=sibling, device_id_type=MESH,
        )

    def level1(t, far):
        places = pl.ds(2 * far, 2)
        return pltpu.make_async_remote_copy(
            src_ref=s1.at[t, e, places], dst_ref=r1.at[t, places],
            send_sem=send1.at[t, far], recv_sem=recv1.at[t, far],
            device_id=partner, device_id_type=MESH,
        )

    def level2(t, p):
        return pltpu.make_async_remote_copy(
            src_ref=s2.at[t, p - 1], dst_ref=r2.at[p - 1, t],
            send_sem=send2.at[t, p - 1], recv_sem=recv2.at[t, p - 1],
            device_id=at(z + jnp.where(e == 1, p, -p), yx), device_id_type=MESH,
        )

    def stage0(t, slot):
        s0[t] = acc[slot, :, :, other].astype(BF16)
        level0(t).start()

    def stage1(t, slot):
        level0(t).wait_recv()
        for zl2 in range(4):
            for zh2 in range(2):
                lanes = slice(zh2 * half, (zh2 + 1) * half)
                value = acc[slot, :, zl2, core, :, lanes] + r0[t, :, zl2, :, lanes].astype(F32)
                delta = lax.rem(zh2 * 4 + zl2 - (z - e) + 16, 8)
                low = (delta >= 1) & (delta <= 4)
                side = jnp.where(low, 0, 1)
                place = jnp.where(low, delta - 1, lax.rem(8 - delta, 8))
                s1[t, side, place] = value.astype(BF16)
                keep[t, side, place] = value
        for far in (1, 0):
            level1(t, far).start()

    def stage2(t):
        for p in (3, 2, 1, 0):
            if p % 2:
                level1(t, p // 2).wait_recv()
            value = keep[t, 1 - e, p] + r1[t, p].astype(F32)
            if p == 0:
                own[t] = value
            else:
                s2[t, p - 1] = value.astype(BF16)
                level2(t, p).start()

    inner = sectors - 2
    gap = LAG - 2
    def first():
        load_psi.wait()
        for copy in load_ops(1):
            copy.wait()
        compute(1, 0, lambda v, shift: psi[v, 1 - shift])

    if EARLY:
        first()
    pl.semaphore_wait(barrier, 4 + 7 + nyx - 1)
    for zl_from, side in ((3, 0), (0, 1)):
        @pl.when(zl == zl_from)
        def _():
            for hop, to_side in ((0, side), (1, side), (2, 1 - side)):
                for v in range(nvec):
                    source = psi_hbm.at[v, 0 if to_side else sectors - 1, mine]
                    halo(to_side, v, hop, source).start()

    if not EARLY:
        first()
    stage0(0, 0)

    @pl.loop(1, sectors + LAG)
    def _(m):
        @pl.when(m < inner)
        def _():
            t = sector_of(m)
            for copy in load_ops(t):
                copy.wait()
            compute(t, lax.rem(m, 2), lambda v, shift: psi[v, t - shift])
            stage1(m - 1, lax.rem(m - 1, 2))
            stage0(m, lax.rem(m, 2))

        @pl.when(m == inner + gap)
        def _():
            for copy in edge_loads:
                copy.wait()
            for side in range(2):
                share(side).wait_recv()

        @pl.when((m >= inner + gap) & (m < sectors + gap))
        def _():
            n = m - gap
            t = sector_of(n)
            for copy in load_ops(t):
                copy.wait()
            which = n - inner
            compute(t, lax.rem(n, 2), lambda v, shift: edge[which, v, 1 - shift])
            stage0(n, lax.rem(n, 2))

        @pl.when(m == inner)
        def _():
            stage1(m - 1, lax.rem(m - 1, 2))

        @pl.when((m > inner + gap) & (m <= sectors + gap))
        def _():
            n = m - 1 - gap
            stage1(n, lax.rem(n, 2))

        @pl.when((m >= RELAY) & (m < RELAY + nvec) & ((zl == 1) | (zl == 2)))
        def _():
            v = m - RELAY
            halo_in(role, v).wait_recv()
            halo(role, v, 0, edge.at[role, v, 2 * role, mine]).start()

            @pl.when(v == nvec - 1)
            def _():
                share(role).start()

        @pl.when(m >= LAG)
        def _():
            stage2(m - LAG)

        @pl.when(m == inner + gap - 1)
        def _():
            for side in range(2):
                @pl.when((zl == 0) | (zl == 3) | (role != side))
                def _():
                    for v in range(nvec):
                        halo_in(side, v).wait_recv()
                    share(side).start()

    near = jnp.where(lax.rem(e + lax.div(zl, 2), 2) == 1, 0, 1)
    part = blk // 8

    def spread(batch, d):
        y, x = lax.div(yx, 4), lax.rem(yx, 4)
        far = lax.rem(y + lax.div(d, 4), 4) * 4 + lax.rem(x + lax.rem(d, 4), 4)
        return pltpu.make_async_remote_copy(
            src_ref=wsend.at[batch, far], dst_ref=wrecv.at[batch, yx],
            send_sem=send3.at[batch, d], recv_sem=recv3.at[batch, d],
            device_id=at(z, far), device_id_type=MESH,
        )

    def keep_own(batch):
        return pltpu.make_async_copy(
            wsend.at[batch, yx], wrecv.at[batch, yx], self_sem.at[batch]
        )

    for batch in range(2):
        ns = slice(batch * 4, batch * 4 + 4)

        @pl.loop(batch * 4, batch * 4 + 4)
        def _(n):
            for p in range(1, 4):
                level2(n, p).wait_recv()

        @pl.loop(0, nvec)
        def _(v):
            for group in range(2):
                if group == 0:
                    value = own[ns, v] + r2[near, ns, v].astype(F32)
                else:
                    value = r2[1 - near, ns, v].astype(F32) + r2[2, ns, v].astype(F32)
                turn[group] = value.reshape(4 * part, half).T
                for lq in range(2):
                    pieces = [turn[group, pl.ds(lq * 4 + r, nyx, stride=8), :] for r in range(4)]
                    for n4 in range(4):
                        lanes = slice(n4 * part, (n4 + 1) * part)
                        joined = jnp.concatenate([piece[:, lanes] for piece in pieces], axis=1)
                        wide[batch, v * 2 + lq, pl.ds(group * 4 + n4, nyx, stride=8), :] = joined

        for tile in range(6):
            lanes = slice(tile * 128, (tile + 1) * 128)
            wsend[batch, :, :, lanes] = wide[batch, tile].reshape(nyx, 8, 128).astype(BF16)

        for d in sorted(range(1, nyx), key=lambda d: -(min(d // 4, 4 - d // 4) + min(d % 4, 4 - d % 4))):
            spread(batch, jnp.int32(d)).start()

        keep_own(batch).start()

    for batch in range(2):
        keep_own(batch).wait()

        @pl.loop(1, nyx)
        def _(d):
            spread(batch, d).wait_recv()

    for v in range(nvec):
        halo(role, v, 0, edge.at[role, v, 2 * role, mine]).wait_send()

    @pl.when((zl == 0) | (zl == 3))
    def _():
        for hop in (1, 2):
            for v in range(nvec):
                halo(role, v, hop, edge.at[role, v, 2 * role, mine]).wait_send()

    for side in range(2):
        share(side).wait_send()

    @pl.loop(0, sectors)
    def _(n):
        level0(n).wait_send()
        for far in range(2):
            level1(n, far).wait_send()
        for p in range(1, 4):
            level2(n, p).wait_send()

    for batch in range(2):
        @pl.loop(1, nyx)
        def _(d):
            spread(batch, d).wait_send()


def transpose_kernel(rows_ref, out_ref, flat):
    zh = lax.rem(lax.axis_index("sec"), 2)
    blk = out_ref.shape[1]
    row = lax.broadcasted_iota(jnp.int32, (blk, blk), 0)
    col = lax.broadcasted_iota(jnp.int32, (blk, blk), 1)

    turn_n = ((row & 128) >> 5) | (row & 3)
    sector = jnp.where(turn_n < 6, turn_n + 1, jnp.where(turn_n == 6, 0, 7))
    group = jnp.where(zh == 1, 1 - ((row & 4) >> 2), (row & 4) >> 2)
    order = jnp.where(
        col == ((row & 120) << 1) + group * 8 + sector, 1.0, 0.0
    ).astype(BF16)
    for tile in range(out_ref.shape[0] // 128):
        lanes = slice(tile * 128, (tile + 1) * 128)
        for batch in range(2):
            value = rows_ref[batch, :, :, lanes].astype(F32).reshape(128, 128)
            flat[lanes, batch * 128 : (batch + 1) * 128] = value.T.astype(BF16)
    for start in range(0, out_ref.shape[0], blk):
        rows = slice(start, start + blk)
        out_ref[rows] = jnp.dot(flat[rows], order, preferred_element_type=F32).astype(BF16)


def solution(mesh):
    nsec = mesh.shape["sec"]
    nyx = nsec // 2

    def per_device(psi, left_ops, right_ops, shifts, active):
        nvec, sectors, blk = psi.shape[:3]
        count = left_ops.shape[0]
        part, half = blk // 8, blk // 2
        sizes = (nyx, count, nvec, sectors, blk)
        smem = pl.BlockSpec(memory_space=pltpu.SMEM)
        hbm = pl.BlockSpec(memory_space=pl.ANY)
        dma = pltpu.SemaphoreType.DMA
        result = pl.pallas_call(
            functools.partial(kernel, nsec * sectors, sizes),
            out_shape=jax.ShapeDtypeStruct((2, nyx, 8, nvec * blk), BF16),
            in_specs=[smem, smem, hbm, hbm, hbm],
            out_specs=hbm,
            scratch_shapes=[
                pltpu.VMEM((nvec, sectors, blk, blk), BF16),
                pltpu.VMEM((2, nvec, 3, blk, blk), BF16),
                pltpu.VMEM((sectors, count, blk, blk), BF16),
                pltpu.VMEM((sectors, count, blk, blk), BF16),
                pltpu.VMEM((blk, blk), BF16),
                pltpu.VMEM((nvec, blk, count * blk), BF16),
                pltpu.VMEM((blk, count * blk), BF16),
                pltpu.VMEM((2, nvec, 4, 2, part, blk), F32),
                pltpu.VMEM((sectors, nvec, 4, part, blk), BF16),
                pltpu.VMEM((sectors, nvec, 4, part, blk), BF16),
                pltpu.VMEM((sectors, 2, 4, nvec, part, half), BF16),
                pltpu.VMEM((sectors, 2, 4, nvec, part, half), F32),
                pltpu.VMEM((sectors, 4, nvec, part, half), BF16),
                pltpu.VMEM((sectors, 3, nvec, part, half), BF16),
                pltpu.VMEM((sectors, nvec, part, half), F32),
                pltpu.VMEM((3, sectors, nvec, part, half), BF16),
                pltpu.VMEM((2, 128, 128), F32),
                pltpu.VMEM((2, nvec * 2, nyx * 8, 128), F32),
                pltpu.VMEM((2, nyx, 8, nvec * blk), BF16),
                dma,
                dma((2, sectors)),
                dma((2,)),
                dma((3, nvec)), dma((2, nvec)), dma((2,)), dma((2,)),
                dma((sectors,)), dma((sectors,)), dma((sectors, 2)), dma((sectors, 2)),
                dma((sectors, 3)), dma((sectors, 3)),
                dma((2, nyx)), dma((2, nyx)),
                dma((2,)),
            ],
            compiler_params=pltpu.CompilerParams(
                collective_id=0, has_side_effects=True, vmem_limit_bytes=56 * 1024 * 1024
            ),
        )(shifts, active, psi, left_ops, right_ops)
        result = pl.pallas_call(
            transpose_kernel,
            out_shape=jax.ShapeDtypeStruct((nvec * blk, blk), BF16),
            in_specs=[pl.BlockSpec(memory_space=pltpu.VMEM)],
            out_specs=pl.BlockSpec(memory_space=pltpu.VMEM),
            scratch_shapes=[pltpu.VMEM((nvec * blk, blk), BF16)],
        )(result)
        return result.reshape(nvec, blk // nsec, blk // 8, blk).transpose(0, 1, 3, 2)

    return jax.shard_map(
        per_device,
        mesh=mesh,
        in_specs=(
            P(None, "sec", None, None),
            P("op", "sec", None, None),
            P("op", "sec", None, None),
            P("op"),
            P("op", "sec"),
        ),
        out_specs=P(None, "sec", None, "op"),
        check_vma=False,
    )
```
